32 devices in a mesh: dp: 8 (over z, core), seq: 4 (over y, x).
Axes of the slice: x: 2, y: 2, z: 4, core: 2. Of those that a mesh axis runs over, the one named last changes fastest.
Arguments:
- latents: bfloat16 [16, 2048, 1152], P('dp', 'seq'), may hold values from -60 to 60, as said below
- cond: bfloat16 [16, 1152], P('dp'), may hold values from -6 to 6
- w_ada: bfloat16 [1152, 6912], P('dp'), may hold values from -0.1875 to 0.1875
- w_qkv: bfloat16 [1152, 3456], P('dp'), may hold values from -1 to 1
- w_proj: bfloat16 [1152, 1152], P('dp'), may hold values from -3 to 3
- w_fc1: bfloat16 [1152, 4608], P('dp'), may hold values from -0.1875 to 0.1875
- w_fc2: bfloat16 [4608, 1152], P('dp'), may hold values from -0.09375 to 0.09375
- cotangent: bfloat16 [16, 2048, 1152], P('dp', 'seq'), may hold values from -6 to 6
Outputs:
- mixed: float32 [16, 2048, 1152], P('dp', 'seq')
- grad_latents: float32 [16, 2048, 1152], P('dp', 'seq')
- grad_cond: float32 [16, 1152], P('dp')
- grad_ada: float32 [1152, 6912], P('dp')
- grad_qkv: float32 [1152, 3456], P('dp')
- grad_proj: float32 [1152, 1152], P('dp')
- grad_fc1: float32 [1152, 4608], P('dp')
- grad_fc2: float32 [4608, 1152], P('dp')
The draws below stay inside these ranges and needn't reach their ends.
Inputs may be any that keep to these rules, and one draw needn't show every extreme that they name: latents of order one, with per-token and per-feature scales.
All inputs are finite; a program needn't handle non-finite values.
Results may differ from the reference program's by a relative error of at most 0.011.
The reference program's roundings to bfloat16 on the way count: a program that leaves them out, or rounds other values in their place, can miss the bound.
Values may be sent and summed in bfloat16 or wider, within the bound.
No kernel may reach another device: no remote copies, remote signals or barrier semaphores. Data moves between devices by JAX's collectives and lax.ppermute only.
A program may use at most 320 MiB of HBM per device.

```python
import math
import jax
import jax.numpy as jnp
from jax import lax

D = 1152
HEADS = 16
HEAD_DIM = 72
FF = 4608
LENGTH = 2048
IMAGES = 16


def draw_latents(key, part):
    key_vals, key_rows, key_cols = jax.random.split(key, 3)
    half = 0.5 * math.log(10.0)
    row_scale = jnp.exp(jax.random.uniform(key_rows, (IMAGES, LENGTH, 1), jnp.float32, -half, half))
    col_scale = jnp.exp(jax.random.uniform(key_cols, (1, 1, D), jnp.float32, -half, half))
    values = jnp.clip(jax.random.normal(key_vals, (IMAGES, LENGTH, D), jnp.float32), -5.5, 5.5)
    return (values * row_scale * col_scale).astype(jnp.bfloat16)


def draw_w_qkv(key, part):
    key_query, key_keys, key_values = jax.random.split(key, 3)
    inverse = 1.0 / math.sqrt(D)
    square = (D, D)
    w_query = jnp.clip(jax.random.normal(key_query, square, jnp.float32), -5.0, 5.0) * inverse
    w_keys = jnp.clip(jax.random.normal(key_keys, square, jnp.float32), -5.0, 5.0) * inverse
    w_values = jnp.clip(jax.random.normal(key_values, square, jnp.float32), -5.0, 5.0) * inverse
    return jnp.clip(jnp.concatenate([w_query, w_keys, w_values], axis=1), -1.0, 1.0).astype(jnp.bfloat16)


def steps_of(key, dims, cuts, low, high):
    factor_of, own = 1.0, jax.random.fold_in(key, 6)
    for axis_at, shards_of in cuts:
        draws = jnp.exp(jax.random.uniform(jax.random.fold_in(own, axis_at), (shards_of,), jnp.float32, low / len(cuts), high / len(cuts)))
        factor_of = factor_of * jnp.repeat(draws, dims[axis_at] // shards_of).reshape([-1 if axis == axis_at else 1 for axis in range(len(dims))])
    return factor_of


def gaussian(own_key, dims, scale, reach, cuts=(), kind=jnp.bfloat16):
    factor_of = steps_of(own_key, dims, cuts, -0.22, 0.18) if cuts else 1.0
    values = jax.random.normal(own_key, dims, jnp.float32) * scale * factor_of
    return jnp.minimum(jnp.maximum(values, -reach), reach).astype(kind)


def setup_inputs(seed: int = 0) -> dict:
    keys = jax.random.split(jax.random.key(seed), 9)
    latents = draw_latents(jax.random.fold_in(keys[8], 71), 0)
    cond = gaussian(keys[1], (IMAGES, D), 1.0, 6.0, ((0, 8),))
    w_ada = gaussian(keys[2], (D, 6 * D), D ** -0.5, 0.1875, ((0, 8),))
    w_qkv = draw_w_qkv(jax.random.fold_in(keys[8], 71), 0)
    w_proj = gaussian(keys[4], (D, D), (max(2, D * 8 // LENGTH)) ** -0.5, 3.0, ((0, 8),))
    w_fc1 = gaussian(keys[5], (D, FF), D ** -0.5, 0.1875, ((0, 8),))
    w_fc2 = gaussian(keys[6], (FF, D), FF ** -0.5, 0.09375, ((0, 8),))
    cotangent = gaussian(keys[7], (IMAGES, LENGTH, D), 1.0, 6.0, ((0, 8), (1, 4)))
    return dict(latents=latents, cond=cond, w_ada=w_ada, w_qkv=w_qkv, w_proj=w_proj, w_fc1=w_fc1, w_fc2=w_fc2, cotangent=cotangent)


@jax.custom_vjp
def low(v):
    return lax.optimization_barrier(v.astype(jnp.bfloat16)).astype(jnp.float32)

@jax.custom_vjp
def low_back(v):
    return v

def low_keep(v):
    return (low(v), None)

def low_pass(kept, grad):
    return (grad,)

def back_keep(v):
    return (v, None)

def back_low(kept, grad):
    return (low(grad),)
low.defvjp(low_keep, low_pass)
low_back.defvjp(back_keep, back_low)
norm_eps = 1e-06
highest = lax.Precision.HIGHEST

def layer_norm(values):
    centre = lax.optimization_barrier(jnp.mean(values, axis=-1, keepdims=True))
    centred = values - centre
    variance = lax.optimization_barrier(jnp.mean(centred * centred, axis=-1, keepdims=True))
    return centred * lax.rsqrt(variance + norm_eps)

def product(former, latter):
    return jnp.dot(former, latter, precision=highest, preferred_element_type=jnp.float32)

def attend_image(queries, keys_all, values_all):
    block_rows = min(512, LENGTH)
    score_scale = 1.0 / math.sqrt(HEAD_DIM)
    query_blocks = queries.reshape(LENGTH // block_rows, block_rows, HEADS, HEAD_DIM)

    def one_block(query_block):
        scores = jnp.einsum('qhd,khd->hqk', query_block, keys_all, precision=highest) * score_scale
        scores = low_back(scores)
        top_score = lax.optimization_barrier(jnp.max(scores, axis=-1, keepdims=True))
        exponent = jnp.exp(scores - top_score)
        weights = low(exponent / lax.optimization_barrier(jnp.sum(exponent, axis=-1, keepdims=True)))
        return jnp.einsum('hqk,khd->qhd', weights, values_all, precision=highest)
    blocks_out = lax.map(jax.checkpoint(one_block), query_blocks)
    return blocks_out.reshape(LENGTH, D)

def image_layer(x_image, mod_image, w_qkv, w_proj, w_fc1, w_fc2):
    shift_one, scale_one, gate_one, shift_two, scale_two, gate_two = jnp.split(mod_image, 6)
    normed_one = low(layer_norm(x_image) * (1.0 + scale_one) + shift_one)
    projected = low(low_back(product(normed_one, w_qkv)))
    queries = projected[:, :D].reshape(LENGTH, HEADS, HEAD_DIM)
    keys_all = projected[:, D:2 * D].reshape(LENGTH, HEADS, HEAD_DIM)
    values_all = projected[:, 2 * D:].reshape(LENGTH, HEADS, HEAD_DIM)
    attended = low(low_back(attend_image(queries, keys_all, values_all)))
    branch_one = low_back(product(attended, w_proj))
    residual = x_image + gate_one * branch_one
    normed_two = low(layer_norm(residual) * (1.0 + scale_two) + shift_two)
    hidden_pre = low_back(product(normed_two, w_fc1))
    hidden_act = low(jax.nn.gelu(hidden_pre, approximate=True))
    branch_two = low_back(product(hidden_act, w_fc2))
    return residual + gate_two * branch_two

def forward(latents, cond, w_ada, w_qkv, w_proj, w_fc1, w_fc2):
    shrunk = low(jax.nn.silu(cond))
    modulation = product(shrunk, w_ada)

    def image_step(x_image, mod_image):
        return image_layer(x_image, mod_image, w_qkv, w_proj, w_fc1, w_fc2)
    checked = jax.checkpoint(image_step)

    def scan_step(carry, pair):
        return (carry, checked(pair[0], pair[1]))
    unused, mixed = lax.scan(scan_step, jnp.zeros((), jnp.float32), (latents, modulation))
    return mixed

def reference(latents, cond, w_ada, w_qkv, w_proj, w_fc1, w_fc2, cotangent):
    inputs = (latents.astype(jnp.float32), cond.astype(jnp.float32), w_ada.astype(jnp.float32), w_qkv.astype(jnp.float32), w_proj.astype(jnp.float32), w_fc1.astype(jnp.float32), w_fc2.astype(jnp.float32))
    mixed, pullback = jax.vjp(forward, *inputs)
    gradients = pullback(cotangent.astype(jnp.float32))
    return (mixed, gradients[0], gradients[1], gradients[2], gradients[3], gradients[4], gradients[5], gradients[6])
```

```python
import functools
import math

import jax
import jax.numpy as jnp
from jax import lax
from jax.experimental import pallas as pl
from jax.experimental.pallas import tpu as pltpu
from jax.sharding import PartitionSpec as P

HEADS = 16
IMAGE_GROUPS = 2

norm_eps = 1e-06
gelu_coeff = 0.044715
log2_e = math.log2(math.e)
half = jnp.bfloat16
full = jnp.float32


def normalize(values):
    centre = jnp.mean(values, axis=-1, keepdims=True)
    centred = values - centre
    variance = jnp.mean(centred * centred, axis=-1, keepdims=True)
    inv_std = lax.rsqrt(variance + norm_eps)
    return (centred * inv_std, inv_std)


def norm_back(grad_hat, scaled, inv_std):
    mean_grad = jnp.mean(grad_hat, axis=-1, keepdims=True)
    mean_cross = jnp.mean(grad_hat * scaled, axis=-1, keepdims=True)
    return (grad_hat - mean_grad - scaled * mean_cross) * inv_std


def dot(former, latter, former_dim, latter_dim):
    return lax.dot_general(
        former, latter, (((former_dim,), (latter_dim,)), ((), ())), preferred_element_type=full
    )


def gelu_parts(hidden_pre):
    factor = math.sqrt(2.0 / math.pi)
    tangent = jnp.tanh(factor * (hidden_pre + gelu_coeff * hidden_pre**3))
    gelu_value = 0.5 * hidden_pre * (1.0 + tangent)
    gelu_slope = 0.5 * (1.0 + tangent) + 0.5 * hidden_pre * (1.0 - tangent * tangent) * factor * (
        1.0 + 3.0 * gelu_coeff * hidden_pre * hidden_pre
    )
    return (gelu_value, gelu_slope)


def split_two(values):
    upper = values.astype(half)
    return upper, (values - upper.astype(full)).astype(half)


def forward_kernel(rows, chunk, q_ref, k_ref, v_ref, o_ref, l_ref, twice_ref, score_ref):
    features, length = k_ref.shape[1:]
    factor = log2_e / math.sqrt(features)
    keys = k_ref[0]
    twice_ref[...] = jnp.concatenate([keys, keys], axis=0).astype(full).T.astype(half)

    def step(at, carry):
        cols = pl.ds(pl.multiple_of(at * rows, rows), rows)
        queries = jnp.concatenate(split_two(q_ref[0, :, cols].astype(full) * factor), axis=0)
        top = None
        for low in range(0, length, chunk):
            scores = dot(twice_ref[low : low + chunk, :], queries, 1, 0)
            score_ref[low : low + chunk, :] = scores
            part = jnp.max(scores.reshape(chunk // 8, 8, rows), axis=0)
            top = part if top is None else jnp.maximum(top, part)
        top = jnp.max(top, axis=0, keepdims=True)
        total = None
        mix = None
        for low in range(0, length, chunk):
            exponent = jnp.exp2(score_ref[low : low + chunk, :] - top)
            part = jnp.sum(exponent.reshape(chunk // 8, 8, rows), axis=0)
            total = part if total is None else total + part
            term = dot(v_ref[0, :, low : low + chunk], exponent.astype(half), 1, 0)
            mix = term if mix is None else mix + term
        total = jnp.sum(total, axis=0, keepdims=True)
        o_ref[0, :, cols] = (mix / total).astype(o_ref.dtype)
        l_ref[0, :, cols] = top + jnp.log2(total)
        return carry

    lax.fori_loop(0, length // rows, step, 0)


def block_of(features, length, offset):
    return pl.BlockSpec((1, features, length), lambda head: (head + offset, 0, 0))


def attend(packed):
    triple, features, length = packed.shape
    heads = triple // 3
    rows, chunk = min(1024, length), min(512, length)
    block = functools.partial(block_of, features, length)
    return pl.pallas_call(
        functools.partial(forward_kernel, rows, chunk),
        grid=(heads,),
        out_shape=(
            jax.ShapeDtypeStruct((heads, features, length), half),
            jax.ShapeDtypeStruct((heads, 1, length), full),
        ),
        in_specs=[block(0), block(heads), block(2 * heads)],
        out_specs=(block(0), block_of(1, length, 0)),
        scratch_shapes=[
            pltpu.VMEM((length, 2 * features), half),
            pltpu.VMEM((length, rows), full),
        ],
        compiler_params=pltpu.CompilerParams(vmem_limit_bytes=40 * 2**20),
        cost_estimate=pl.CostEstimate(
            flops=14 * heads * length * length * features,
            bytes_accessed=8 * heads * length * features,
            transcendentals=heads * length * length,
        ),
        name="attend",
    )(packed, packed, packed)


def backward_kernel(
    rows, chunk, q_ref, k_ref, v_ref, g_ref, l_ref, out_ref, k_s, twice_s, dk_s, dv_s, p_s, t_s
):
    features, length = k_ref.shape[1:]
    scale = 1.0 / math.sqrt(features)
    factor = log2_e * scale
    keys = k_ref[0]
    row_id = lax.broadcasted_iota(jnp.int32, (8, length), 0)
    ones = jnp.where(row_id < 3, 1.0, 0.0).astype(half)
    twice_s[...] = jnp.concatenate([keys, keys, ones], axis=0)
    lanes = k_s.shape[1]
    wide = jnp.concatenate([keys.astype(full), jnp.zeros((lanes - features, length), full)], axis=0)
    k_s[...] = wide.T.astype(half)
    dk_s[...] = jnp.zeros_like(dk_s)
    dv_s[...] = jnp.zeros_like(dv_s)

    def step(at, carry):
        cols = pl.ds(pl.multiple_of(at * rows, rows), rows)
        queries = q_ref[0, :, cols]
        grads = g_ref[0, :, cols]
        upper, lower = split_two(queries.astype(full) * factor)
        rest = -l_ref[0, :, cols]
        first = rest.astype(half).astype(full)
        second = (rest - first).astype(half).astype(full)
        third = rest - first - second
        which = lax.broadcasted_iota(jnp.int32, (8, rows), 0)
        extra = jnp.where(
            which == 0, first, jnp.where(which == 1, second, jnp.where(which == 2, third, 0.0))
        ).astype(half)
        wide_queries = jnp.concatenate([upper, lower, extra], axis=0)
        centre = None
        for low in range(0, length, chunk):
            span = slice(low, low + chunk)
            prob = jnp.exp2(dot(wide_queries, twice_s[:, span], 0, 0))
            p_s[:, span] = prob
            both = prob * dot(grads, v_ref[0, :, span], 0, 0)
            t_s[:, span] = both
            for lane in range(0, chunk, 128):
                part = both[:, lane : lane + 128]
                centre = part if centre is None else centre + part
        centre = jnp.sum(centre, axis=1, keepdims=True)
        dq = None
        for low in range(0, length, chunk):
            span = slice(low, low + chunk)
            prob = p_s[:, span]
            dv_s[:, span] += dot(grads, prob.astype(half), 1, 0)
            grad_scores = (t_s[:, span] - prob * centre).astype(half)
            dk_s[:, span] += dot(queries, grad_scores, 1, 0)
            term = dot(grad_scores, k_s[span, :], 1, 0)
            dq = term if dq is None else dq + term
        out_ref[0, 0, :, cols] = (dq * scale).T[:features].astype(half)
        return carry

    lax.fori_loop(0, length // rows, step, 0)
    out_ref[1, 0] = (dk_s[...] * scale).astype(half)
    out_ref[2, 0] = dv_s[...].astype(half)


def attend_back(packed, grads, log_totals):
    triple, features, length = packed.shape
    heads = triple // 3
    rows, chunk = min(512, length), min(256, length)
    lanes = -(-features // 128) * 128
    block = functools.partial(block_of, features, length)
    return pl.pallas_call(
        functools.partial(backward_kernel, rows, chunk),
        grid=(heads,),
        out_shape=jax.ShapeDtypeStruct((3, heads, features, length), half),
        in_specs=[block(0), block(heads), block(2 * heads), block(0), block_of(1, length, 0)],
        out_specs=pl.BlockSpec((3, 1, features, length), lambda head: (0, head, 0, 0)),
        scratch_shapes=[
            pltpu.VMEM((length, lanes), half),
            pltpu.VMEM((2 * features + 8, length), half),
            pltpu.VMEM((features, length), full),
            pltpu.VMEM((features, length), full),
            pltpu.VMEM((rows, length), full),
            pltpu.VMEM((rows, length), full),
        ],
        compiler_params=pltpu.CompilerParams(vmem_limit_bytes=40 * 2**20),
        cost_estimate=pl.CostEstimate(
            flops=28 * heads * length * length * features,
            bytes_accessed=16 * heads * length * features,
            transcendentals=heads * length * length,
        ),
        name="attend_back",
    )(packed, packed, packed, grads, log_totals)


class Exchange:
    def __init__(self):
        self.size = lax.axis_size("seq")
        self.groups = self.size // IMAGE_GROUPS
        index = lax.axis_index("seq")
        self.side = index % IMAGE_GROUPS
        self.group = index // IMAGE_GROUPS

    def across(self, value):
        return lax.ppermute(value, "seq", [(at, at ^ 1) for at in range(self.size)])

    def shift(self, value, by):
        pairs = [
            (2 * group + side, 2 * ((group + by) % self.groups) + side)
            for group in range(self.groups)
            for side in range(2)
        ]
        return lax.ppermute(value, "seq", pairs)

    def total(self, value):
        value = value + self.across(value)
        return value + sum(self.shift(value, by) for by in range(1, self.groups))

    def mine(self, first, second):
        return jnp.where(self.side == 0, first, second)

    def other(self, first, second):
        return jnp.where(self.side == 0, second, first)


def gather_rows(shard):
    return lax.all_gather(shard, "dp", axis=0, tiled=True)


def scatter_rows(term):
    return lax.psum_scatter(term, "dp", scatter_dimension=0, tiled=True)


def per_device(latents, cond, w_ada, w_qkv, w_proj, w_fc1, w_fc2, cotangent):
    ex = Exchange()
    groups = ex.groups
    dp_size = lax.axis_size("dp")
    dp_index = lax.axis_index("dp")
    images_here, tokens_here, width = latents.shape
    flat_rows = images_here * tokens_here
    length = ex.size * tokens_here
    features = width // HEADS
    span = width // groups
    own_heads = HEADS // groups
    ada_rows = w_ada.shape[0]

    cond_all = gather_rows(cond).astype(full)
    logistic_all = jax.nn.sigmoid(cond_all)
    shrunk_all = (cond_all * logistic_all).astype(half)
    shrunk_rows = lax.dynamic_slice_in_dim(shrunk_all, dp_index * ada_rows, ada_rows, 1)
    mod_terms = dot(shrunk_rows, w_ada, 1, 0)
    mod_terms = lax.all_to_all(mod_terms, "dp", split_axis=0, concat_axis=0, tiled=True)
    modulation = jnp.sum(mod_terms.reshape(dp_size, images_here, 6 * width), axis=0)
    shift_one, scale_one, gate_one, shift_two, scale_two, gate_two = [
        piece[:, None, :] for piece in jnp.split(modulation, 6, axis=1)
    ]

    received = ex.across(ex.other(latents[0], latents[1]))
    pair = jnp.concatenate([ex.mine(latents[0], latents[1]), received], axis=0)
    tokens_image = jnp.concatenate([pair] + [ex.shift(pair, by) for by in range(1, groups)], axis=0)

    qkv_cols = lax.dynamic_slice_in_dim(
        w_qkv.reshape(w_qkv.shape[0], 3, width), ex.group * span, span, 2
    ).reshape(w_qkv.shape[0], 3 * span)
    qkv_full = gather_rows(qkv_cols)
    proj_full = gather_rows(w_proj)
    fc1_full = gather_rows(w_fc1)
    fc2_full = gather_rows(w_fc2)

    hat_image, _ = normalize(tokens_image.astype(full))
    normed_image = (
        hat_image * (1.0 + ex.mine(scale_one[0], scale_one[1]))
        + ex.mine(shift_one[0], shift_one[1])
    ).astype(half)
    packed = dot(qkv_full, normed_image, 0, 1).astype(half)
    packed = packed.reshape(3 * own_heads, features, length)
    attended_own, log_totals = attend(packed)
    attended_own = attended_own.reshape(span, groups, 2 * tokens_here)

    attended_pair = jnp.zeros((width, 2 * tokens_here), half)
    for by in range(groups):
        block = attended_own[:, by]
        block = ex.shift(block, -by) if by else block
        start = ((ex.group + by) % groups) * span
        attended_pair = lax.dynamic_update_slice_in_dim(attended_pair, block, start, 0)
    kept, sent = attended_pair[:, :tokens_here], attended_pair[:, tokens_here:]
    received = ex.across(sent)
    attended = jnp.concatenate([ex.mine(kept, received), ex.other(kept, received)], axis=1)

    latent_full = latents.astype(full)
    branch_one = dot(attended, proj_full, 0, 0).reshape(images_here, tokens_here, width)
    residual = latent_full + gate_one * branch_one
    hat_two, inv_two = normalize(residual)
    normed_two = (hat_two * (1.0 + scale_two) + shift_two).astype(half).reshape(flat_rows, width)
    hidden_pre = dot(normed_two, fc1_full, 1, 0)
    gelu_value, gelu_slope = gelu_parts(hidden_pre)
    hidden_act = gelu_value.astype(half)
    branch_two = dot(hidden_act, fc2_full, 1, 0).reshape(images_here, tokens_here, width)
    mixed = residual + gate_two * branch_two

    grad_out = cotangent.astype(full)
    grad_gate_two = jnp.sum(grad_out * branch_two, axis=1)
    grad_branch_two = (grad_out * gate_two).astype(half).reshape(flat_rows, width)
    grad_act = dot(grad_branch_two, fc2_full, 1, 1)
    grad_pre = (grad_act * gelu_slope).astype(half)
    grad_normed_two = dot(grad_pre, fc1_full, 1, 1).reshape(images_here, tokens_here, width)
    grad_shift_two = jnp.sum(grad_normed_two, axis=1)
    grad_scale_two = jnp.sum(grad_normed_two * hat_two, axis=1)
    grad_residual = grad_out + norm_back(grad_normed_two * (1.0 + scale_two), hat_two, inv_two)
    grad_gate_one = jnp.sum(grad_residual * branch_one, axis=1)
    grad_branch_one = (grad_residual * gate_one).astype(half).reshape(flat_rows, width)
    grad_attended = dot(proj_full, grad_branch_one, 1, 1).astype(half)

    first, second = grad_attended[:, :tokens_here], grad_attended[:, tokens_here:]
    received = ex.across(ex.other(first, second))
    grad_pair = jnp.concatenate([ex.mine(first, second), received], axis=1)
    blocks = []
    for by in range(groups):
        start = ((ex.group + by) % groups) * span
        block = lax.dynamic_slice_in_dim(grad_pair, start, span, 0)
        blocks.append(ex.shift(block, by) if by else block)
    grad_heads = jnp.concatenate(blocks, axis=1).reshape(own_heads, features, length)

    grad_fc2 = scatter_rows(dot(hidden_act, grad_branch_two, 0, 0).astype(half))
    grad_fc1 = scatter_rows(dot(normed_two, grad_pre, 0, 0).astype(half))
    grad_proj = scatter_rows(dot(attended, grad_branch_one, 1, 0).astype(half))
    grad_fc2 = lax.psum(grad_fc2.astype(full), "seq")
    grad_fc1 = lax.psum(grad_fc1.astype(full), "seq")
    grad_proj = lax.psum(grad_proj.astype(full), "seq")

    grad_packed = attend_back(packed, grad_heads, log_totals).reshape(3 * span, length)

    grad_qkv = scatter_rows(dot(normed_image, grad_packed, 0, 1).astype(half))
    grad_qkv = lax.all_gather(grad_qkv, "seq", axis=0).astype(full)
    qkv_rows = w_qkv.shape[0]
    grad_qkv = jnp.sum(grad_qkv.reshape(groups, 2, qkv_rows, 3, span), axis=1)
    grad_qkv = jnp.transpose(grad_qkv, (1, 2, 0, 3)).reshape(qkv_rows, 3 * width)

    terms = dot(grad_packed, qkv_full, 0, 1)
    terms = terms.reshape(groups, 2 * tokens_here, width)
    grad_pair_normed = terms[0]
    for by in range(1, groups):
        grad_pair_normed = grad_pair_normed + ex.shift(terms[by].astype(half), -by).astype(full)
    kept = grad_pair_normed[:tokens_here]
    received = ex.across(grad_pair_normed[tokens_here:].astype(half)).astype(full)
    grad_normed_one = jnp.stack([ex.mine(kept, received), ex.other(kept, received)])

    hat_one, inv_one = normalize(latent_full)
    grad_shift_one = jnp.sum(grad_normed_one, axis=1)
    grad_scale_one = jnp.sum(grad_normed_one * hat_one, axis=1)
    grad_latents = grad_residual + norm_back(grad_normed_one * (1.0 + scale_one), hat_one, inv_one)

    late = ex.total(jnp.concatenate([grad_shift_one, grad_scale_one], axis=1))
    early = ex.total(
        jnp.concatenate([grad_gate_one, grad_shift_two, grad_scale_two, grad_gate_two], axis=1)
    )
    shrunk_own = shrunk_rows.astype(full)
    grad_ada = []
    grad_shrunk = 0.0
    for piece, low in ((late, 0), (early, 2 * width)):
        piece = gather_rows(piece)
        grad_ada.append(
            lax.dot_general(
                shrunk_own,
                piece,
                (((0,), (0,)), ((), ())),
                precision=lax.Precision.HIGHEST,
                preferred_element_type=full,
            )
        )
        upper, lower = split_two(piece)
        ada_cols = w_ada[:, low : low + piece.shape[1]]
        grad_shrunk = grad_shrunk + dot(upper, ada_cols, 1, 1) + dot(lower, ada_cols, 1, 1)
    grad_ada = jnp.concatenate(grad_ada, axis=1)
    grad_shrunk = lax.all_to_all(grad_shrunk, "dp", split_axis=0, concat_axis=0, tiled=True)
    grad_shrunk = grad_shrunk.reshape(dp_size, images_here, ada_rows)
    grad_shrunk = jnp.transpose(grad_shrunk, (1, 0, 2)).reshape(images_here, width)
    cond_full = cond.astype(full)
    logistic = jax.nn.sigmoid(cond_full)
    grad_cond = grad_shrunk * logistic * (1.0 + cond_full * (1.0 - logistic))
    return (
        mixed,
        grad_latents,
        grad_cond,
        grad_ada,
        grad_qkv,
        grad_proj,
        grad_fc1,
        grad_fc2,
    )


def solution(mesh):
    tokens = P("dp", "seq", None)
    rows = P("dp", None)
    return jax.shard_map(
        per_device,
        mesh=mesh,
        in_specs=(tokens, rows, rows, rows, rows, rows, rows, tokens),
        out_specs=(tokens, tokens, rows, rows, rows, rows, rows, rows),
        check_vma=False,
    )
```

```python
import functools
import math

import jax
import jax.numpy as jnp
from jax import lax
from jax.experimental import pallas as pl
from jax.experimental.pallas import tpu as pltpu
from jax.sharding import PartitionSpec as P

HEADS = 16
IMAGE_GROUPS = 2

norm_eps = 1e-06
gelu_coeff = 0.044715
log2_e = math.log2(math.e)
half = jnp.bfloat16
full = jnp.float32


def normalize(values):
    centre = jnp.mean(values, axis=-1, keepdims=True)
    centred = values - centre
    variance = jnp.mean(centred * centred, axis=-1, keepdims=True)
    inv_std = lax.rsqrt(variance + norm_eps)
    return (centred * inv_std, inv_std)


def norm_back(grad_hat, scaled, inv_std):
    mean_grad = jnp.mean(grad_hat, axis=-1, keepdims=True)
    mean_cross = jnp.mean(grad_hat * scaled, axis=-1, keepdims=True)
    return (grad_hat - mean_grad - scaled * mean_cross) * inv_std


def dot(former, latter, former_dim, latter_dim):
    return lax.dot_general(
        former, latter, (((former_dim,), (latter_dim,)), ((), ())), preferred_element_type=full
    )


def gelu_parts(hidden_pre):
    factor = math.sqrt(2.0 / math.pi)
    tangent = jnp.tanh(factor * (hidden_pre + gelu_coeff * hidden_pre**3))
    gelu_value = 0.5 * hidden_pre * (1.0 + tangent)
    gelu_slope = 0.5 * (1.0 + tangent) + 0.5 * hidden_pre * (1.0 - tangent * tangent) * factor * (
        1.0 + 3.0 * gelu_coeff * hidden_pre * hidden_pre
    )
    return (gelu_value, gelu_slope)


def split_two(values):
    upper = values.astype(half)
    return upper, (values - upper.astype(full)).astype(half)


def forward_kernel(rows, chunk, q_ref, k_ref, v_ref, o_ref, l_ref, twice_ref, score_ref):
    steps_each = o_ref.shape[3] // rows
    features, length = k_ref.shape[1:]
    factor = log2_e / math.sqrt(features)
    keys = k_ref[0]
    twice_ref[...] = jnp.concatenate([keys, keys], axis=0).astype(full).T.astype(half)

    def step(at, carry):
        cols = pl.ds(pl.multiple_of(at * rows, rows), rows)
        queries = jnp.concatenate(split_two(q_ref[0, :, cols].astype(full) * factor), axis=0)
        top = None
        for low in range(0, length, chunk):
            scores = dot(twice_ref[low : low + chunk, :], queries, 1, 0)
            score_ref[low : low + chunk, :] = scores
            part = jnp.max(scores.reshape(chunk // 8, 8, rows), axis=0)
            top = part if top is None else jnp.maximum(top, part)
        top = jnp.max(top, axis=0, keepdims=True)
        total = None
        mix = None
        for low in range(0, length, chunk):
            exponent = jnp.exp2(score_ref[low : low + chunk, :] - top)
            part = jnp.sum(exponent.reshape(chunk // 8, 8, rows), axis=0)
            total = part if total is None else total + part
            term = dot(v_ref[0, :, low : low + chunk], exponent.astype(half), 1, 0)
            mix = term if mix is None else mix + term
        total = jnp.sum(total, axis=0, keepdims=True)
        within = pl.ds(pl.multiple_of((at % steps_each) * rows, rows), rows)
        o_ref[at // steps_each, 0, :, within] = (mix / total).astype(o_ref.dtype)
        l_ref[0, :, cols] = top + jnp.log2(total)
        return carry

    lax.fori_loop(0, length // rows, step, 0)


def block_of(features, length, offset):
    return pl.BlockSpec((1, features, length), lambda head: (head + offset, 0, 0))


def attend(packed, heads, which, groups):
    features, length = packed.shape[1:]
    each = length // groups
    rows, chunk = min(1024, each), min(512, length)
    block = functools.partial(block_of, features, length)
    base = 3 * heads * which
    return pl.pallas_call(
        functools.partial(forward_kernel, rows, chunk),
        grid=(heads,),
        out_shape=(
            jax.ShapeDtypeStruct((groups, heads, features, each), half),
            jax.ShapeDtypeStruct((heads, 1, length), full),
        ),
        in_specs=[block(base), block(base + heads), block(base + 2 * heads)],
        out_specs=(
            pl.BlockSpec((groups, 1, features, each), lambda head: (0, head, 0, 0)),
            block_of(1, length, 0),
        ),
        scratch_shapes=[
            pltpu.VMEM((length, 2 * features), half),
            pltpu.VMEM((length, rows), full),
        ],
        compiler_params=pltpu.CompilerParams(vmem_limit_bytes=40 * 2**20),
        cost_estimate=pl.CostEstimate(
            flops=14 * heads * length * length * features,
            bytes_accessed=8 * heads * length * features,
            transcendentals=heads * length * length,
        ),
        name="attend",
    )(packed, packed, packed)


def backward_kernel(
    rows, chunk, q_ref, k_ref, v_ref, g_ref, l_ref, *refs
):
    out_ref, k_s, twice_s, dk_s, dv_s, p_s, t_s = refs[-7:]
    features, length = k_ref.shape[1:]
    scale = 1.0 / math.sqrt(features)
    factor = log2_e * scale
    keys = k_ref[0]
    row_id = lax.broadcasted_iota(jnp.int32, (8, length), 0)
    ones = jnp.where(row_id < 3, 1.0, 0.0).astype(half)
    twice_s[...] = jnp.concatenate([keys, keys, ones], axis=0)
    lanes = k_s.shape[1]
    wide = jnp.concatenate([keys.astype(full), jnp.zeros((lanes - features, length), full)], axis=0)
    k_s[...] = wide.T.astype(half)
    dk_s[...] = jnp.zeros_like(dk_s)
    dv_s[...] = jnp.zeros_like(dv_s)

    def step(at, carry):
        cols = pl.ds(pl.multiple_of(at * rows, rows), rows)
        queries = q_ref[0, :, cols]
        grads = g_ref[0, :, cols]
        upper, lower = split_two(queries.astype(full) * factor)
        rest = -l_ref[0, :, cols]
        first = rest.astype(half).astype(full)
        second = (rest - first).astype(half).astype(full)
        third = rest - first - second
        which = lax.broadcasted_iota(jnp.int32, (8, rows), 0)
        extra = jnp.where(
            which == 0, first, jnp.where(which == 1, second, jnp.where(which == 2, third, 0.0))
        ).astype(half)
        wide_queries = jnp.concatenate([upper, lower, extra], axis=0)
        centre = None
        for low in range(0, length, chunk):
            span = slice(low, low + chunk)
            prob = jnp.exp2(dot(wide_queries, twice_s[:, span], 0, 0))
            p_s[:, span] = prob
            both = prob * dot(grads, v_ref[0, :, span], 0, 0)
            t_s[:, span] = both
            for lane in range(0, chunk, 128):
                part = both[:, lane : lane + 128]
                centre = part if centre is None else centre + part
        centre = jnp.sum(centre, axis=1, keepdims=True)
        dq = None
        for low in range(0, length, chunk):
            span = slice(low, low + chunk)
            prob = p_s[:, span]
            dv_s[:, span] += dot(grads, prob.astype(half), 1, 0)
            grad_scores = (t_s[:, span] - prob * centre).astype(half)
            dk_s[:, span] += dot(queries, grad_scores, 1, 0)
            term = dot(grad_scores, k_s[span, :], 1, 0)
            dq = term if dq is None else dq + term
        out_ref[0, 0, :, cols] = (dq * scale).T[:features].astype(half)
        return carry

    lax.fori_loop(0, length // rows, step, 0)
    out_ref[1, 0] = (dk_s[...] * scale).astype(half)
    out_ref[2, 0] = dv_s[...].astype(half)


def attend_back(packed, grads, log_totals, heads, which, earlier):
    features, length = packed.shape[1:]
    rows, chunk = min(512, length), min(256, length)
    lanes = -(-features // 128) * 128
    block = functools.partial(block_of, features, length)
    base = 3 * heads * which
    operands = [packed, packed, packed, grads, log_totals]
    in_specs = [block(base), block(base + heads), block(base + 2 * heads), block(heads * which)]
    in_specs.append(block_of(1, length, 0))
    aliases = {}
    if earlier is not None:
        aliases = {len(operands): 0}
        operands.append(earlier)
        in_specs.append(pl.BlockSpec(memory_space=pl.ANY))
    return pl.pallas_call(
        functools.partial(backward_kernel, rows, chunk),
        grid=(heads,),
        out_shape=jax.ShapeDtypeStruct((packed.shape[0] // heads, heads, features, length), half),
        in_specs=in_specs,
        out_specs=pl.BlockSpec((3, 1, features, length), lambda head: (which, head, 0, 0)),
        input_output_aliases=aliases,
        scratch_shapes=[
            pltpu.VMEM((length, lanes), half),
            pltpu.VMEM((2 * features + 8, length), half),
            pltpu.VMEM((features, length), full),
            pltpu.VMEM((features, length), full),
            pltpu.VMEM((rows, length), full),
            pltpu.VMEM((rows, length), full),
        ],
        compiler_params=pltpu.CompilerParams(vmem_limit_bytes=40 * 2**20),
        cost_estimate=pl.CostEstimate(
            flops=28 * heads * length * length * features,
            bytes_accessed=16 * heads * length * features,
            transcendentals=heads * length * length,
        ),
        name="attend_back",
    )(*operands)


class Exchange:
    def __init__(self):
        self.size = lax.axis_size("seq")
        self.groups = self.size // IMAGE_GROUPS
        index = lax.axis_index("seq")
        self.side = index % IMAGE_GROUPS
        self.group = index // IMAGE_GROUPS

    def across(self, value):
        return lax.ppermute(value, "seq", [(at, at ^ 1) for at in range(self.size)])

    def shift(self, value, by):
        pairs = [
            (2 * group + side, 2 * ((group + by) % self.groups) + side)
            for group in range(self.groups)
            for side in range(2)
        ]
        return lax.ppermute(value, "seq", pairs)

    def over_groups(self, value):
        sent = value.astype(self.kind(value))
        for by in range(1, self.groups):
            value = value + self.shift(sent, by).astype(full)
        return value

    def over_sides(self, value):
        return value + self.across(value.astype(self.kind(value))).astype(full)

    def kind(self, value):
        return half if value.size > 65536 else full

    def total(self, value):
        return self.over_groups(self.over_sides(value.astype(full)))

    def place(self, values, at):
        return jnp.concatenate([lax.dynamic_index_in_dim(values, spot, 0) for spot in at], axis=0)

    def mine(self, first, second):
        return jnp.where(self.side == 0, first, second)

    def other(self, first, second):
        return jnp.where(self.side == 0, second, first)


def gather_rows(shard):
    return lax.all_gather(shard, "dp", axis=0, tiled=True)


def scatter_rows(term):
    return lax.psum_scatter(term, "dp", scatter_dimension=0, tiled=True)


def per_device(latents, cond, w_ada, w_qkv, w_proj, w_fc1, w_fc2, cotangent):
    ex = Exchange()
    groups = ex.groups
    dp_size = lax.axis_size("dp")
    dp_index = lax.axis_index("dp")
    images_here, tokens_here, width = latents.shape
    flat_rows = images_here * tokens_here
    length = ex.size * tokens_here
    features = width // HEADS
    span = width // groups
    own_heads = HEADS // groups
    chunks = 2
    chunk_heads = own_heads // chunks
    piece = span // chunks
    ada_rows = w_ada.shape[0]

    cond_full = cond.astype(full)
    logistic = jax.nn.sigmoid(cond_full)
    shrunk = (cond_full * logistic).astype(half).reshape(images_here, dp_size, ada_rows)
    shrunk_rows = lax.all_to_all(jnp.swapaxes(shrunk, 0, 1), "dp", 0, 0)
    shrunk_rows = shrunk_rows.reshape(dp_size * images_here, ada_rows)
    mod_terms = dot(shrunk_rows, w_ada, 1, 0)
    mod_terms = lax.all_to_all(mod_terms, "dp", split_axis=0, concat_axis=0, tiled=True)
    modulation = jnp.sum(mod_terms.reshape(dp_size, images_here, 6 * width), axis=0)
    shift_one, scale_one, gate_one, shift_two, scale_two, gate_two = [
        piece[:, None, :] for piece in jnp.split(modulation, 6, axis=1)
    ]

    own = ex.mine(latents[0], latents[1])
    received = ex.across(ex.other(latents[0], latents[1]))
    blocks = [own, received]
    for by in range(1, groups):
        blocks += [ex.shift(own, by), ex.shift(received, by)]
    tokens_image = jnp.concatenate(blocks, axis=0)

    starts = [
        part * width + ex.group * span + which * piece
        for which in range(chunks)
        for part in range(3)
    ]
    qkv_cols = jnp.concatenate(
        [lax.dynamic_slice_in_dim(w_qkv, start, piece, 1) for start in starts], axis=1
    )
    qkv_full = gather_rows(qkv_cols)
    proj_full = gather_rows(w_proj)
    fc1_full = gather_rows(w_fc1)
    fc2_full = gather_rows(w_fc2)
    proj_full = ex.place(
        proj_full.reshape(groups, span, width), [(ex.group + by) % groups for by in range(groups)]
    ).reshape(width, width)

    hat_image, _ = normalize(tokens_image.astype(full))
    normed_image = (
        hat_image * (1.0 + ex.mine(scale_one[0], scale_one[1]))
        + ex.mine(shift_one[0], shift_one[1])
    ).astype(half)
    packed = dot(qkv_full, normed_image, 0, 1).astype(half)
    packed = packed.reshape(3 * own_heads, features, length)

    log_totals = []
    pieces = {}
    for which in range(chunks):
        attended_own, log_total = attend(packed, chunk_heads, which, groups)
        log_totals.append(log_total)
        attended_own = attended_own.reshape(groups, piece, 2 * tokens_here)
        for by in range(groups):
            block = ex.shift(attended_own[by], -by) if by else attended_own[0]
            received = ex.across(block[:, tokens_here:])
            kept = block[:, :tokens_here]
            pieces[by, which] = jnp.concatenate(
                [ex.mine(kept, received), ex.other(kept, received)], axis=1
            )
    attended = jnp.concatenate(
        [pieces[by, which] for by in range(groups) for which in range(chunks)], axis=0
    )

    latent_full = latents.astype(full)
    branch_one = dot(attended, proj_full, 0, 0).reshape(images_here, tokens_here, width)
    residual = latent_full + gate_one * branch_one
    hat_two, inv_two = normalize(residual)
    normed_two = (hat_two * (1.0 + scale_two) + shift_two).astype(half).reshape(flat_rows, width)
    hidden_pre = dot(normed_two, fc1_full, 1, 0)
    gelu_value, gelu_slope = gelu_parts(hidden_pre)
    hidden_act = gelu_value.astype(half)
    branch_two = dot(hidden_act, fc2_full, 1, 0).reshape(images_here, tokens_here, width)
    mixed = residual + gate_two * branch_two

    grad_out = cotangent.astype(full)
    grad_gate_two = jnp.sum(grad_out * branch_two, axis=1)
    grad_branch_two = (grad_out * gate_two).astype(half).reshape(flat_rows, width)
    grad_act = dot(grad_branch_two, fc2_full, 1, 1)
    grad_pre = (grad_act * gelu_slope).astype(half)
    grad_normed_two = dot(grad_pre, fc1_full, 1, 1).reshape(images_here, tokens_here, width)
    grad_shift_two = jnp.sum(grad_normed_two, axis=1)
    grad_scale_two = jnp.sum(grad_normed_two * hat_two, axis=1)
    grad_residual = grad_out + norm_back(grad_normed_two * (1.0 + scale_two), hat_two, inv_two)
    grad_gate_one = jnp.sum(grad_residual * branch_one, axis=1)
    grad_branch_one = (grad_residual * gate_one).astype(half).reshape(flat_rows, width)
    grad_attended = dot(proj_full, grad_branch_one, 1, 1).astype(half)

    first, second = grad_attended[:, :tokens_here], grad_attended[:, tokens_here:]
    received = ex.across(ex.other(first, second))
    own = ex.mine(first, second)
    term_fc2 = dot(hidden_act, grad_branch_two, 0, 0).astype(half)
    early = ex.total(
        jnp.concatenate([grad_gate_one, grad_shift_two, grad_scale_two, grad_gate_two], axis=1)
    )
    own_moved = [ex.shift(own[by * span : (by + 1) * span], by) for by in range(1, groups)]
    received, term_fc2 = lax.optimization_barrier((received, term_fc2))
    grad_fc2 = scatter_rows(term_fc2)
    received_moved = [ex.shift(received[by * span : (by + 1) * span], by) for by in range(1, groups)]
    term_fc1 = dot(normed_two, grad_pre, 0, 0).astype(half)
    term_proj = dot(attended, grad_branch_one, 1, 0).astype(half)
    term_proj = ex.place(
        term_proj.reshape(groups, span, width), [(by - ex.group) % groups for by in range(groups)]
    ).reshape(width, width)
    early = gather_rows(early)
    received_moved, own_moved, term_fc1, term_proj, early = lax.optimization_barrier(
        (received_moved, own_moved, term_fc1, term_proj, early)
    )
    grad_fc1 = scatter_rows(term_fc1)
    blocks = [own[:span], received[:span]]
    for by in range(1, groups):
        blocks += [own_moved[by - 1], received_moved[by - 1]]
    grad_heads = jnp.concatenate(blocks, axis=1).reshape(own_heads, features, length)

    grad_packed = None
    for which in range(chunks):
        grad_packed = attend_back(
            packed, grad_heads, log_totals[which], chunk_heads, which, grad_packed
        )
    grad_packed = grad_packed.reshape(3 * span, length)
    grad_packed, grad_fc2 = lax.optimization_barrier((grad_packed, grad_fc2))
    grad_fc2 = ex.total(grad_fc2)

    def term_of(at):
        return dot(grad_packed[:, at * tokens_here : (at + 1) * tokens_here], qkv_full, 0, 1)

    partner_term, own_term = 0.0, 0.0
    for by in range(1, groups):
        partner_term += ex.shift(term_of(2 * by + 1).astype(half), -by).astype(full)
    for by in range(1, groups):
        own_term += ex.shift(term_of(2 * by).astype(half), -by).astype(full)
    received = ex.across((partner_term + term_of(1)).astype(half)).astype(full)
    kept = own_term + term_of(0)
    grad_normed_one = jnp.stack([ex.mine(kept, received), ex.other(kept, received)])

    grad_qkv = scatter_rows(dot(normed_image, grad_packed, 0, 1).astype(half))
    grad_proj = ex.total(scatter_rows(term_proj))
    grad_fc1 = ex.total(grad_fc1)
    grad_qkv = ex.over_sides(grad_qkv.astype(full)).astype(half)
    grad_qkv = jnp.stack([grad_qkv] + [ex.shift(grad_qkv, by) for by in range(1, groups)])
    grad_qkv = ex.place(grad_qkv, [(ex.group - at) % groups for at in range(groups)])
    qkv_rows = w_qkv.shape[0]
    grad_qkv = grad_qkv.reshape(groups, qkv_rows, chunks, 3, piece)
    grad_qkv = jnp.concatenate(
        [
            grad_qkv[at, :, which, part]
            for part in range(3)
            for at in range(groups)
            for which in range(chunks)
        ],
        axis=1,
    ).astype(full)

    hat_one, inv_one = normalize(latent_full)
    grad_shift_one = jnp.sum(grad_normed_one, axis=1)
    grad_scale_one = jnp.sum(grad_normed_one * hat_one, axis=1)
    grad_latents = grad_residual + norm_back(grad_normed_one * (1.0 + scale_one), hat_one, inv_one)

    late = gather_rows(ex.total(jnp.concatenate([grad_shift_one, grad_scale_one], axis=1)))
    shrunk_own = shrunk_rows.astype(full)
    grad_ada = []
    grad_shrunk = 0.0
    for sums, low in ((late, 0), (early, 2 * width)):
        grad_ada.append(
            lax.dot_general(
                shrunk_own,
                sums,
                (((0,), (0,)), ((), ())),
                precision=lax.Precision.HIGHEST,
                preferred_element_type=full,
            )
        )
        upper, lower = split_two(sums)
        ada_cols = w_ada[:, low : low + sums.shape[1]]
        grad_shrunk = grad_shrunk + dot(upper, ada_cols, 1, 1) + dot(lower, ada_cols, 1, 1)
    grad_ada = jnp.concatenate(grad_ada, axis=1)
    grad_shrunk = lax.all_to_all(grad_shrunk, "dp", split_axis=0, concat_axis=0, tiled=True)
    grad_shrunk = grad_shrunk.reshape(dp_size, images_here, ada_rows)
    grad_shrunk = jnp.transpose(grad_shrunk, (1, 0, 2)).reshape(images_here, width)
    grad_cond = grad_shrunk * logistic * (1.0 + cond_full * (1.0 - logistic))
    return (
        mixed,
        grad_latents,
        grad_cond,
        grad_ada,
        grad_qkv,
        grad_proj,
        grad_fc1,
        grad_fc2,
    )


def solution(mesh):
    tokens = P("dp", "seq", None)
    rows = P("dp", None)
    return jax.shard_map(
        per_device,
        mesh=mesh,
        in_specs=(tokens, rows, rows, rows, rows, rows, rows, tokens),
        out_specs=(tokens, tokens, rows, rows, rows, rows, rows, rows),
        check_vma=False,
    )
```

```python
import functools
import math

import jax
import jax.numpy as jnp
from jax import lax
from jax.experimental import pallas as pl
from jax.experimental.pallas import tpu as pltpu
from jax.sharding import PartitionSpec as P

HEADS = 16
IMAGE_GROUPS = 2

norm_eps = 1e-06
gelu_coeff = 0.044715
log2_e = math.log2(math.e)
half = jnp.bfloat16
full = jnp.float32


def normalize(values):
    centre = jnp.mean(values, axis=-1, keepdims=True)
    centred = values - centre
    variance = jnp.mean(centred * centred, axis=-1, keepdims=True)
    inv_std = lax.rsqrt(variance + norm_eps)
    return (centred * inv_std, inv_std)


def norm_back(grad_hat, scaled, inv_std):
    mean_grad = jnp.mean(grad_hat, axis=-1, keepdims=True)
    mean_cross = jnp.mean(grad_hat * scaled, axis=-1, keepdims=True)
    return (grad_hat - mean_grad - scaled * mean_cross) * inv_std


def dot(former, latter, former_dim, latter_dim):
    return lax.dot_general(
        former, latter, (((former_dim,), (latter_dim,)), ((), ())), preferred_element_type=full
    )


def gelu_parts(hidden_pre):
    factor = math.sqrt(2.0 / math.pi)
    tangent = jnp.tanh(factor * (hidden_pre + gelu_coeff * hidden_pre**3))
    gelu_value = 0.5 * hidden_pre * (1.0 + tangent)
    gelu_slope = 0.5 * (1.0 + tangent) + 0.5 * hidden_pre * (1.0 - tangent * tangent) * factor * (
        1.0 + 3.0 * gelu_coeff * hidden_pre * hidden_pre
    )
    return (gelu_value, gelu_slope)


def split_two(values):
    upper = values.astype(half)
    return upper, (values - upper.astype(full)).astype(half)


def forward_kernel(rows, chunk, q_ref, k_ref, v_ref, o_ref, l_ref, twice_ref, score_ref):
    steps_each = o_ref.shape[3] // rows
    features, length = k_ref.shape[1:]
    factor = log2_e / math.sqrt(features)
    keys = k_ref[0]
    twice_ref[...] = jnp.concatenate([keys, keys], axis=0).astype(full).T.astype(half)

    def step(at, carry):
        cols = pl.ds(pl.multiple_of(at * rows, rows), rows)
        queries = jnp.concatenate(split_two(q_ref[0, :, cols].astype(full) * factor), axis=0)
        top = None
        for low in range(0, length, chunk):
            scores = dot(twice_ref[low : low + chunk, :], queries, 1, 0)
            score_ref[low : low + chunk, :] = scores
            part = jnp.max(scores.reshape(chunk // 8, 8, rows), axis=0)
            top = part if top is None else jnp.maximum(top, part)
        top = jnp.max(top, axis=0, keepdims=True)
        total = None
        mix = None
        for low in range(0, length, chunk):
            exponent = jnp.exp2(score_ref[low : low + chunk, :] - top)
            part = jnp.sum(exponent.reshape(chunk // 8, 8, rows), axis=0)
            total = part if total is None else total + part
            term = dot(v_ref[0, :, low : low + chunk], exponent.astype(half), 1, 0)
            mix = term if mix is None else mix + term
        total = jnp.sum(total, axis=0, keepdims=True)
        within = pl.ds(pl.multiple_of((at % steps_each) * rows, rows), rows)
        o_ref[at // steps_each, 0, :, within] = (mix / total).astype(o_ref.dtype)
        l_ref[0, :, cols] = top + jnp.log2(total)
        return carry

    lax.fori_loop(0, length // rows, step, 0)


def block_of(features, length, offset):
    return pl.BlockSpec((1, features, length), lambda head: (head + offset, 0, 0))


def attend(packed, heads, which, groups):
    features, length = packed.shape[1:]
    each = length // groups
    rows, chunk = min(1024, each), min(512, length)
    block = functools.partial(block_of, features, length)
    base = 3 * heads * which
    return pl.pallas_call(
        functools.partial(forward_kernel, rows, chunk),
        grid=(heads,),
        out_shape=(
            jax.ShapeDtypeStruct((groups, heads, features, each), half),
            jax.ShapeDtypeStruct((heads, 1, length), full),
        ),
        in_specs=[block(base), block(base + heads), block(base + 2 * heads)],
        out_specs=(
            pl.BlockSpec((groups, 1, features, each), lambda head: (0, head, 0, 0)),
            block_of(1, length, 0),
        ),
        scratch_shapes=[
            pltpu.VMEM((length, 2 * features), half),
            pltpu.VMEM((length, rows), full),
        ],
        compiler_params=pltpu.CompilerParams(vmem_limit_bytes=40 * 2**20),
        cost_estimate=pl.CostEstimate(
            flops=14 * heads * length * length * features,
            bytes_accessed=8 * heads * length * features,
            transcendentals=heads * length * length,
        ),
        name="attend",
    )(packed, packed, packed)


def backward_kernel(
    rows, chunk, q_ref, k_ref, v_ref, g_ref, l_ref, *refs
):
    out_ref, k_s, twice_s, dk_s, dv_s, p_s, t_s = refs[-7:]
    features, length = k_ref.shape[1:]
    scale = 1.0 / math.sqrt(features)
    factor = log2_e * scale
    keys = k_ref[0]
    row_id = lax.broadcasted_iota(jnp.int32, (8, length), 0)
    ones = jnp.where(row_id < 3, 1.0, 0.0).astype(half)
    twice_s[...] = jnp.concatenate([keys, keys, ones], axis=0)
    lanes = k_s.shape[1]
    wide = jnp.concatenate([keys.astype(full), jnp.zeros((lanes - features, length), full)], axis=0)
    k_s[...] = wide.T.astype(half)
    dk_s[...] = jnp.zeros_like(dk_s)
    dv_s[...] = jnp.zeros_like(dv_s)

    def step(at, carry):
        cols = pl.ds(pl.multiple_of(at * rows, rows), rows)
        queries = q_ref[0, :, cols]
        grads = g_ref[0, :, cols]
        upper, lower = split_two(queries.astype(full) * factor)
        rest = -l_ref[0, :, cols]
        first = rest.astype(half).astype(full)
        second = (rest - first).astype(half).astype(full)
        third = rest - first - second
        which = lax.broadcasted_iota(jnp.int32, (8, rows), 0)
        extra = jnp.where(
            which == 0, first, jnp.where(which == 1, second, jnp.where(which == 2, third, 0.0))
        ).astype(half)
        wide_queries = jnp.concatenate([upper, lower, extra], axis=0)
        centre = None
        for low in range(0, length, chunk):
            span = slice(low, low + chunk)
            prob = jnp.exp2(dot(wide_queries, twice_s[:, span], 0, 0))
            p_s[:, span] = prob
            both = prob * dot(grads, v_ref[0, :, span], 0, 0)
            t_s[:, span] = both
            for lane in range(0, chunk, 128):
                part = both[:, lane : lane + 128]
                centre = part if centre is None else centre + part
        centre = jnp.sum(centre, axis=1, keepdims=True)
        dq = None
        for low in range(0, length, chunk):
            span = slice(low, low + chunk)
            prob = p_s[:, span]
            dv_s[:, span] += dot(grads, prob.astype(half), 1, 0)
            grad_scores = (t_s[:, span] - prob * centre).astype(half)
            dk_s[:, span] += dot(queries, grad_scores, 1, 0)
            term = dot(grad_scores, k_s[span, :], 1, 0)
            dq = term if dq is None else dq + term
        out_ref[0, 0, :, cols] = (dq * scale).T[:features].astype(half)
        return carry

    lax.fori_loop(0, length // rows, step, 0)
    out_ref[1, 0] = (dk_s[...] * scale).astype(half)
    out_ref[2, 0] = dv_s[...].astype(half)


def attend_back(packed, grads, log_totals, heads, which, earlier):
    features, length = packed.shape[1:]
    rows, chunk = min(512, length), min(256, length)
    lanes = -(-features // 128) * 128
    block = functools.partial(block_of, features, length)
    base = 3 * heads * which
    operands = [packed, packed, packed, grads, log_totals]
    in_specs = [block(base), block(base + heads), block(base + 2 * heads), block(heads * which)]
    in_specs.append(block_of(1, length, 0))
    aliases = {}
    if earlier is not None:
        aliases = {len(operands): 0}
        operands.append(earlier)
        in_specs.append(pl.BlockSpec(memory_space=pl.ANY))
    return pl.pallas_call(
        functools.partial(backward_kernel, rows, chunk),
        grid=(heads,),
        out_shape=jax.ShapeDtypeStruct((packed.shape[0] // heads, heads, features, length), half),
        in_specs=in_specs,
        out_specs=pl.BlockSpec((3, 1, features, length), lambda head: (which, head, 0, 0)),
        input_output_aliases=aliases,
        scratch_shapes=[
            pltpu.VMEM((length, lanes), half),
            pltpu.VMEM((2 * features + 8, length), half),
            pltpu.VMEM((features, length), full),
            pltpu.VMEM((features, length), full),
            pltpu.VMEM((rows, length), full),
            pltpu.VMEM((rows, length), full),
        ],
        compiler_params=pltpu.CompilerParams(vmem_limit_bytes=40 * 2**20),
        cost_estimate=pl.CostEstimate(
            flops=28 * heads * length * length * features,
            bytes_accessed=16 * heads * length * features,
            transcendentals=heads * length * length,
        ),
        name="attend_back",
    )(*operands)


class Exchange:
    def __init__(self):
        self.size = lax.axis_size("seq")
        self.groups = self.size // IMAGE_GROUPS
        index = lax.axis_index("seq")
        self.side = index % IMAGE_GROUPS
        self.group = index // IMAGE_GROUPS

    def across(self, value):
        return lax.ppermute(value, "seq", [(at, at ^ 1) for at in range(self.size)])

    def shift(self, value, by):
        pairs = [
            (2 * group + side, 2 * ((group + by) % self.groups) + side)
            for group in range(self.groups)
            for side in range(2)
        ]
        return lax.ppermute(value, "seq", pairs)

    def over_groups(self, value):
        sent = value.astype(self.kind(value))
        for by in range(1, self.groups):
            value = value + self.shift(sent, by).astype(full)
        return value

    def over_sides(self, value):
        return value + self.across(value.astype(self.kind(value))).astype(full)

    def kind(self, value):
        return half if value.size > 65536 else full

    def total(self, value):
        return self.over_groups(self.over_sides(value.astype(full)))

    def place(self, values, at):
        return jnp.concatenate([lax.dynamic_index_in_dim(values, spot, 0) for spot in at], axis=0)

    def mine(self, first, second):
        return jnp.where(self.side == 0, first, second)

    def other(self, first, second):
        return jnp.where(self.side == 0, second, first)


def gather_rows(shard):
    return lax.all_gather(shard, "dp", axis=0, tiled=True)


def scatter_rows(term):
    return lax.psum_scatter(term, "dp", scatter_dimension=0, tiled=True)


def per_device(latents, cond, w_ada, w_qkv, w_proj, w_fc1, w_fc2, cotangent):
    ex = Exchange()
    groups = ex.groups
    dp_size = lax.axis_size("dp")
    dp_index = lax.axis_index("dp")
    images_here, tokens_here, width = latents.shape
    flat_rows = images_here * tokens_here
    length = ex.size * tokens_here
    features = width // HEADS
    span = width // groups
    own_heads = HEADS // groups
    chunks = 2
    chunk_heads = own_heads // chunks
    piece = span // chunks
    ada_rows = w_ada.shape[0]

    cond_full = cond.astype(full)
    logistic = jax.nn.sigmoid(cond_full)
    shrunk = (cond_full * logistic).astype(half).reshape(images_here, dp_size, ada_rows)
    shrunk_rows = lax.all_to_all(jnp.swapaxes(shrunk, 0, 1), "dp", 0, 0)
    shrunk_rows = shrunk_rows.reshape(dp_size * images_here, ada_rows)
    mod_terms = dot(shrunk_rows, w_ada, 1, 0)
    mod_terms = lax.all_to_all(mod_terms, "dp", split_axis=0, concat_axis=0, tiled=True)
    modulation = jnp.sum(mod_terms.reshape(dp_size, images_here, 6 * width), axis=0)
    shift_one, scale_one, gate_one, shift_two, scale_two, gate_two = [
        piece[:, None, :] for piece in jnp.split(modulation, 6, axis=1)
    ]

    own = ex.mine(latents[0], latents[1])
    received = ex.across(ex.other(latents[0], latents[1]))
    blocks = [own, received]
    for by in range(1, groups):
        blocks += [ex.shift(own, by), ex.shift(received, by)]
    tokens_image = jnp.concatenate(blocks, axis=0)

    starts = [
        part * width + ex.group * span + which * piece
        for which in range(chunks)
        for part in range(3)
    ]
    qkv_cols = jnp.concatenate(
        [lax.dynamic_slice_in_dim(w_qkv, start, piece, 1) for start in starts], axis=1
    )
    qkv_full = gather_rows(qkv_cols)
    proj_full = gather_rows(w_proj)
    fc1_full = gather_rows(w_fc1)
    fc2_full = gather_rows(w_fc2)
    proj_full = ex.place(
        proj_full.reshape(groups, span, width), [(ex.group + by) % groups for by in range(groups)]
    ).reshape(width, width)

    hat_image, _ = normalize(tokens_image.astype(full))
    normed_image = (
        hat_image * (1.0 + ex.mine(scale_one[0], scale_one[1]))
        + ex.mine(shift_one[0], shift_one[1])
    ).astype(half)
    packed = dot(qkv_full, normed_image, 0, 1).astype(half)
    packed = packed.reshape(3 * own_heads, features, length)

    log_totals = []
    pieces = {}
    for which in range(chunks):
        attended_own, log_total = attend(packed, chunk_heads, which, groups)
        log_totals.append(log_total)
        attended_own = attended_own.reshape(groups, piece, 2 * tokens_here)
        for by in range(groups):
            block = ex.shift(attended_own[by], -by) if by else attended_own[0]
            received = ex.across(block[:, tokens_here:])
            kept = block[:, :tokens_here]
            pieces[by, which] = jnp.concatenate(
                [ex.mine(kept, received), ex.other(kept, received)], axis=1
            )
    attended = jnp.concatenate(
        [pieces[by, which] for by in range(groups) for which in range(chunks)], axis=0
    )

    latent_full = latents.astype(full)
    branch_one = dot(attended, proj_full, 0, 0).reshape(images_here, tokens_here, width)
    residual = latent_full + gate_one * branch_one
    hat_two, inv_two = normalize(residual)
    normed_two = (hat_two * (1.0 + scale_two) + shift_two).astype(half).reshape(flat_rows, width)
    hidden_pre = dot(normed_two, fc1_full, 1, 0)
    gelu_value, gelu_slope = gelu_parts(hidden_pre)
    hidden_act = gelu_value.astype(half)
    branch_two = dot(hidden_act, fc2_full, 1, 0).reshape(images_here, tokens_here, width)
    mixed = residual + gate_two * branch_two

    grad_out = cotangent.astype(full)
    grad_gate_two = jnp.sum(grad_out * branch_two, axis=1)
    grad_branch_two = (grad_out * gate_two).astype(half).reshape(flat_rows, width)
    grad_act = dot(grad_branch_two, fc2_full, 1, 1)
    grad_pre = (grad_act * gelu_slope).astype(half)
    grad_normed_two = dot(grad_pre, fc1_full, 1, 1).reshape(images_here, tokens_here, width)
    grad_shift_two = jnp.sum(grad_normed_two, axis=1)
    grad_scale_two = jnp.sum(grad_normed_two * hat_two, axis=1)
    grad_residual = grad_out + norm_back(grad_normed_two * (1.0 + scale_two), hat_two, inv_two)
    grad_gate_one = jnp.sum(grad_residual * branch_one, axis=1)
    grad_branch_one = (grad_residual * gate_one).astype(half).reshape(flat_rows, width)
    grad_attended = dot(proj_full, grad_branch_one, 1, 1).astype(half)

    grad_attended, late_branch_one = lax.optimization_barrier((grad_attended, grad_branch_one))
    first, second = grad_attended[:, :tokens_here], grad_attended[:, tokens_here:]
    received = ex.across(ex.other(first, second))
    own = ex.mine(first, second)
    term_fc2 = dot(hidden_act, grad_branch_two, 0, 0).astype(half)
    early = ex.total(
        jnp.concatenate([grad_gate_one, grad_shift_two, grad_scale_two, grad_gate_two], axis=1)
    )
    own_moved = [ex.shift(own[by * span : (by + 1) * span], by) for by in range(1, groups)]
    grad_fc2 = scatter_rows(term_fc2)
    received_moved = [ex.shift(received[by * span : (by + 1) * span], by) for by in range(1, groups)]
    term_fc1 = dot(normed_two, grad_pre, 0, 0).astype(half)
    grad_fc1 = scatter_rows(term_fc1)
    term_proj = dot(attended, late_branch_one, 1, 0).astype(half)
    term_proj = ex.place(
        term_proj.reshape(groups, span, width), [(by - ex.group) % groups for by in range(groups)]
    ).reshape(width, width)
    early = gather_rows(early)
    received_moved, own_moved, term_proj, early, grad_fc2 = lax.optimization_barrier(
        (received_moved, own_moved, term_proj, early, grad_fc2)
    )
    grad_proj = scatter_rows(term_proj)
    grad_fc2 = ex.over_sides(grad_fc2.astype(full)).astype(half)
    blocks = [own[:span], received[:span]]
    for by in range(1, groups):
        blocks += [own_moved[by - 1], received_moved[by - 1]]
    grad_heads = jnp.concatenate(blocks, axis=1).reshape(own_heads, features, length)

    grad_packed = None
    for which in range(chunks):
        if which:
            grad_packed, grad_fc2, grad_fc1 = lax.optimization_barrier(
                (grad_packed, grad_fc2, grad_fc1)
            )
            grad_fc2 = ex.over_groups(grad_fc2.astype(full))
            grad_fc1 = ex.over_sides(grad_fc1.astype(full)).astype(half)
        grad_packed = attend_back(
            packed, grad_heads, log_totals[which], chunk_heads, which, grad_packed
        )
    grad_packed = grad_packed.reshape(3 * span, length)
    grad_packed, grad_fc2, grad_fc1, grad_proj = lax.optimization_barrier(
        (grad_packed, grad_fc2, grad_fc1, grad_proj)
    )
    grad_fc1 = ex.over_groups(grad_fc1.astype(full))

    def term_of(at):
        return dot(grad_packed[:, at * tokens_here : (at + 1) * tokens_here], qkv_full, 0, 1)

    partner_term, own_term = 0.0, 0.0
    for by in range(1, groups):
        partner_term += ex.shift(term_of(2 * by + 1).astype(half), -by).astype(full)
    for by in range(1, groups):
        own_term += ex.shift(term_of(2 * by).astype(half), -by).astype(full)
    received = ex.across((partner_term + term_of(1)).astype(half)).astype(full)
    kept = own_term + term_of(0)
    grad_normed_one = jnp.stack([ex.mine(kept, received), ex.other(kept, received)])

    grad_qkv = scatter_rows(dot(normed_image, grad_packed, 0, 1).astype(half))
    grad_proj = ex.total(grad_proj)
    grad_qkv = ex.over_sides(grad_qkv.astype(full)).astype(half)
    grad_qkv = jnp.stack([grad_qkv] + [ex.shift(grad_qkv, by) for by in range(1, groups)])
    grad_qkv = ex.place(grad_qkv, [(ex.group - at) % groups for at in range(groups)])
    qkv_rows = w_qkv.shape[0]
    grad_qkv = grad_qkv.reshape(groups, qkv_rows, chunks, 3, piece)
    grad_qkv = jnp.concatenate(
        [
            grad_qkv[at, :, which, part]
            for part in range(3)
            for at in range(groups)
            for which in range(chunks)
        ],
        axis=1,
    ).astype(full)

    hat_one, inv_one = normalize(latent_full)
    grad_shift_one = jnp.sum(grad_normed_one, axis=1)
    grad_scale_one = jnp.sum(grad_normed_one * hat_one, axis=1)
    grad_latents = grad_residual + norm_back(grad_normed_one * (1.0 + scale_one), hat_one, inv_one)

    late = gather_rows(ex.total(jnp.concatenate([grad_shift_one, grad_scale_one], axis=1)))
    shrunk_own = shrunk_rows.astype(full)
    grad_ada = []
    grad_shrunk = 0.0
    for sums, low in ((late, 0), (early, 2 * width)):
        grad_ada.append(
            lax.dot_general(
                shrunk_own,
                sums,
                (((0,), (0,)), ((), ())),
                precision=lax.Precision.HIGHEST,
                preferred_element_type=full,
            )
        )
        upper, lower = split_two(sums)
        ada_cols = w_ada[:, low : low + sums.shape[1]]
        grad_shrunk = grad_shrunk + dot(upper, ada_cols, 1, 1) + dot(lower, ada_cols, 1, 1)
    grad_ada = jnp.concatenate(grad_ada, axis=1)
    grad_shrunk = lax.all_to_all(grad_shrunk, "dp", split_axis=0, concat_axis=0, tiled=True)
    grad_shrunk = grad_shrunk.reshape(dp_size, images_here, ada_rows)
    grad_shrunk = jnp.transpose(grad_shrunk, (1, 0, 2)).reshape(images_here, width)
    grad_cond = grad_shrunk * logistic * (1.0 + cond_full * (1.0 - logistic))
    return (
        mixed,
        grad_latents,
        grad_cond,
        grad_ada,
        grad_qkv,
        grad_proj,
        grad_fc1,
        grad_fc2,
    )


def solution(mesh):
    tokens = P("dp", "seq", None)
    rows = P("dp", None)
    return jax.shard_map(
        per_device,
        mesh=mesh,
        in_specs=(tokens, rows, rows, rows, rows, rows, rows, tokens),
        out_specs=(tokens, tokens, rows, rows, rows, rows, rows, rows),
        check_vma=False,
    )
```
